32 devices in a mesh: rows: 16 (over z, y, x), cols: 2 (over core).
Axes of the slice: x: 2, y: 2, z: 4, core: 2. Of those that a mesh axis runs over, the one named last changes fastest.
Arguments:
- homolog_embedding: bfloat16 [128, 1024, 256], P('rows', 'cols'), may hold values from -120 to 120
- couple_embedding: bfloat16 [1024, 1024, 128], P('rows', 'cols'), may hold values from -6 to 6
- homolog_standardize_factor: float32 [256], replicated, may hold values from 0.25 to 1.75
- first_factor_mapping: bfloat16 [256, 32], replicated, may hold values from -0.375 to 0.375
- second_factor_mapping: bfloat16 [256, 32], replicated, may hold values from -0.375 to 0.375
- contraction_to_couple_mapping: bfloat16 [1024, 128], replicated, may hold values from -2 to 2
- couple_standardize_factor: float32 [128], replicated, may hold values from 0.25 to 1.75
- widening_matrix: bfloat16 [128, 512], replicated, may hold values from -0.5 to 0.5
- narrowing_matrix: bfloat16 [512, 128], replicated, may hold values from -0.25 to 0.25
Outputs:
- pair_out: bfloat16 [1024, 1024, 128], P('rows', 'cols')
The draws below stay inside these ranges and needn't reach their ends.
All inputs are finite; a program needn't handle non-finite values.
Results may differ from the reference program's by a relative error of at most 0.0064.
Values may be sent and summed in bfloat16 or wider, within the bound.
No kernel may reach another device: no remote copies, remote signals or barrier semaphores. Data moves between devices by JAX's collectives and lax.ppermute only.
A program may use at most 128 MiB of HBM per device.

```python
import math
import jax
import jax.numpy as jnp
from jax import lax

FEATURE_DEPTH = 256
FACTOR_DIM = 32
CZ = 128
FFN = 512
CHAIN_LENGTH = 1024
HOMOLOG_COUNT = 128


def draw_homolog_embedding(key, part):
    key_base = jax.random.fold_in(key, 11)
    key_rows = jax.random.fold_in(key, 12)
    random_seed_cols_draw = jax.random.fold_in(key, 13)
    complete_extent = (HOMOLOG_COUNT, CHAIN_LENGTH, FEATURE_DEPTH)
    row_scale = jnp.exp(jax.random.uniform(key_rows, (HOMOLOG_COUNT, CHAIN_LENGTH, 1), jnp.float32, 0.0, math.log(10.0)))
    per_feature_factor = jnp.exp(jax.random.uniform(random_seed_cols_draw, (1, 1, FEATURE_DEPTH), jnp.float32, math.log(0.5), math.log(2.0)))
    sampled_entries = jax.random.truncated_normal(key_base, -6.0, 6.0, complete_extent, jnp.float32)
    return (sampled_entries * per_feature_factor * row_scale).astype(jnp.bfloat16)


def shard_levels(stream_key, dims, split, least, top_value):
    factor_of = 1.0
    for dim, parts in split:
        draws = jax.random.uniform(jax.random.fold_in(jax.random.fold_in(stream_key, 6), dim), (parts,), jnp.float32, least / len(split), top_value / len(split))
        factor_of = factor_of * jnp.repeat(jnp.exp(draws), dims[dim] // parts).reshape((-1,) + (1,) * (len(dims) - 1 - dim))
    return factor_of


def noise(stream_key, extent, width, reach, shards=(), dtype=jnp.bfloat16):
    drawn = jax.random.normal(stream_key, extent, jnp.float32) * width
    if len(shards) > 0:
        drawn = shard_levels(stream_key, extent, shards, -0.22, 0.18) * drawn
    return jnp.clip(drawn, min=-reach, max=reach).astype(dtype)


def setup_inputs(seed: int = 0) -> dict:
    key_list = jax.random.split(jax.random.key(seed), 10)
    return {
        "homolog_embedding": draw_homolog_embedding(jax.random.fold_in(key_list[9], 71), 0),
        "couple_embedding": noise(key_list[1], (CHAIN_LENGTH, CHAIN_LENGTH, CZ), 1.0, 6.0, ((0, 16), (1, 2))),
        "homolog_standardize_factor": jnp.clip(1.0 + 0.15 * jax.random.normal(key_list[2], (FEATURE_DEPTH,), jnp.float32), 0.25, 1.75),
        "first_factor_mapping": noise(key_list[3], (FEATURE_DEPTH, FACTOR_DIM), FEATURE_DEPTH ** -0.5, 0.375),
        "second_factor_mapping": noise(key_list[4], (FEATURE_DEPTH, FACTOR_DIM), FEATURE_DEPTH ** -0.5, 0.375),
        "contraction_to_couple_mapping": noise(key_list[5], (FACTOR_DIM * FACTOR_DIM, CZ), (max(1, FACTOR_DIM * FACTOR_DIM // HOMOLOG_COUNT)) ** -0.5, 2.0),
        "couple_standardize_factor": jnp.clip(1.0 + 0.15 * jax.random.normal(key_list[6], (CZ,), jnp.float32), 0.25, 1.75),
        "widening_matrix": noise(key_list[7], (CZ, FFN), CZ ** -0.5, 0.5),
        "narrowing_matrix": noise(key_list[8], (FFN, CZ), FFN ** -0.5, 0.25),
    }


def standardize_features(sampled_entries, gain_vector):
    floats = sampled_entries.astype(jnp.float32)
    average = lax.optimization_barrier(jnp.mean(floats, axis=-1, keepdims=True))
    centred = floats - average
    variance = lax.optimization_barrier(jnp.mean(centred * centred, axis=-1, keepdims=True))
    return centred * lax.rsqrt(variance + 1e-05) * gain_vector.astype(jnp.float32)

def reference(homolog_embedding, couple_embedding, homolog_standardize_factor, first_factor_mapping, second_factor_mapping, contraction_to_couple_mapping, couple_standardize_factor, widening_matrix, narrowing_matrix):
    standardized_tensor = standardize_features(homolog_embedding, homolog_standardize_factor).astype(jnp.bfloat16)
    unrolled_tensor = standardized_tensor.reshape(HOMOLOG_COUNT * CHAIN_LENGTH, FEATURE_DEPTH)
    left_rows = jnp.dot(unrolled_tensor, first_factor_mapping, preferred_element_type=jnp.float32).astype(jnp.bfloat16).reshape(HOMOLOG_COUNT, CHAIN_LENGTH, FACTOR_DIM)
    right_rows = jnp.dot(unrolled_tensor, second_factor_mapping, preferred_element_type=jnp.float32).astype(jnp.bfloat16).reshape(HOMOLOG_COUNT, CHAIN_LENGTH, FACTOR_DIM)
    block = math.gcd(CHAIN_LENGTH, 16)
    block_count = CHAIN_LENGTH // block
    left_blocks = left_rows.reshape(HOMOLOG_COUNT, block_count, block, FACTOR_DIM).transpose(1, 0, 2, 3)
    right_float = right_rows.astype(jnp.float32)

    def project_block(left_block):
        outer_product = jnp.einsum('sip,sjq->ijpq', left_block.astype(jnp.float32), right_float) / HOMOLOG_COUNT
        outer_product = outer_product.astype(jnp.bfloat16).reshape(block * CHAIN_LENGTH, FACTOR_DIM * FACTOR_DIM)
        return jnp.dot(outer_product, contraction_to_couple_mapping, preferred_element_type=jnp.float32).reshape(block, CHAIN_LENGTH, CZ)
    update = lax.map(project_block, left_blocks).reshape(CHAIN_LENGTH, CHAIN_LENGTH, CZ)
    pair_mid = couple_embedding.astype(jnp.float32) + update
    pair_normed = standardize_features(pair_mid, couple_standardize_factor).astype(jnp.bfloat16).reshape(CHAIN_LENGTH * CHAIN_LENGTH, CZ)
    hidden = jnp.maximum(jnp.dot(pair_normed, widening_matrix, preferred_element_type=jnp.float32), 0.0).astype(jnp.bfloat16)
    result = pair_mid + jnp.dot(hidden, narrowing_matrix, preferred_element_type=jnp.float32).reshape(CHAIN_LENGTH, CHAIN_LENGTH, CZ)
    return result.astype(jnp.bfloat16)
```

```python
import functools
import math

import jax
import jax.numpy as jnp
from jax import lax
from jax.experimental import pallas as pl
from jax.experimental.pallas import tpu as pltpu
from jax.sharding import PartitionSpec as P

LANES = 128
EPS = 1e-05
BF, F32 = jnp.bfloat16, jnp.float32


def whole(array):
    return pl.BlockSpec(array.shape, lambda *_: (0,) * array.ndim, pipeline_mode=pl.Buffered(1))


def front_kernel(x_ref, gain_ref, w_ref, left_ref, right_ref, left_acc, right_acc, *, inner, tile):
    s = pl.program_id(0)
    count = pl.num_programs(0)
    chunks, lanes = right_ref.shape[0], right_ref.shape[2]
    width = w_ref.shape[0] // 2
    group = lanes // tile
    x = x_ref[0].astype(F32)
    mean = jnp.mean(x, axis=-1, keepdims=True)
    d = x - mean
    var = jnp.mean(d * d, axis=-1, keepdims=True)
    normed = (d * lax.rsqrt(var + EPS) * gain_ref[...]).astype(BF)
    y = lax.dot_general(
        w_ref[...], normed, (((1,), (1,)), ((), ())), preferred_element_type=F32
    )
    part = width // group
    for c in range(chunks):
        right_acc[c, pl.ds(s, width, stride=count), :] = y[width:, c * lanes : (c + 1) * lanes]
    for dest in range(left_ref.shape[0] * left_ref.shape[1]):
        row = jnp.concatenate(
            [
                y[t * part : (t + 1) * part, dest * tile : (dest + 1) * tile]
                for t in range(group)
            ],
            axis=1,
        )
        left_acc[dest % inner, dest // inner, pl.ds(s, part, stride=count), :] = row

    @pl.when(s == count - 1)
    def _():
        left_ref[...] = left_acc[...].astype(BF)
        right_ref[...] = right_acc[...].astype(BF)


def front(x, gain, weights, inner, tile):
    seqs, res, depth = x.shape
    width = weights.shape[0] // 2
    dests = res // tile
    group = LANES // tile
    left = (inner, dests // inner, width // group * seqs, LANES)
    right = (res // LANES, width * seqs, LANES)
    return pl.pallas_call(
        functools.partial(front_kernel, inner=inner, tile=tile),
        grid=(seqs,),
        in_specs=[
            pl.BlockSpec((1, res, depth), lambda s: (s, 0, 0)),
            whole(gain),
            whole(weights),
        ],
        out_specs=[
            pl.BlockSpec(left, lambda s: (0,) * 4),
            pl.BlockSpec(right, lambda s: (0,) * 3),
        ],
        out_shape=[jax.ShapeDtypeStruct(left, BF), jax.ShapeDtypeStruct(right, BF)],
        scratch_shapes=[pltpu.VMEM(left, F32), pltpu.VMEM(right, F32)],
        name="front",
    )(x, gain, weights)


def turn_kernel(flag_ref, own_ref, got_ref, out_ref, acc, *, seqs, tile):
    outer, inner, rows, lanes = own_ref.shape
    part = rows // seqs
    group = lanes // tile
    width = part * group
    flag = flag_ref[0] == 1
    for b in range(part):
        x = jnp.concatenate(
            [
                jnp.where(
                    flag,
                    own_ref[z, k, b * seqs : (b + 1) * seqs, :].astype(F32),
                    got_ref[z, k, b * seqs : (b + 1) * seqs, :].astype(F32),
                )
                for k in range(inner)
                for z in range(outer)
            ],
            axis=0,
        )
        xt = x.T
        for t in range(group):
            for c in range(acc.shape[0]):
                acc[c, pl.ds(t * part + b, tile, stride=width), :] = xt[
                    t * tile : (t + 1) * tile, c * LANES : (c + 1) * LANES
                ]
    for c in range(acc.shape[0]):
        out_ref[:, c * LANES : (c + 1) * LANES] = acc[c].astype(BF)


def turn(flag, own, got, seqs, tile):
    outer, inner, rows, lanes = own.shape
    shape = (tile * (rows // seqs) * (lanes // tile), outer * inner * seqs)
    return pl.pallas_call(
        functools.partial(turn_kernel, seqs=seqs, tile=tile),
        in_specs=[pl.BlockSpec(memory_space=pltpu.SMEM)] + [pl.BlockSpec(memory_space=pltpu.VMEM)] * 2,
        out_specs=pl.BlockSpec(memory_space=pltpu.VMEM),
        out_shape=jax.ShapeDtypeStruct(shape, BF),
        scratch_shapes=[pltpu.VMEM((shape[1] // LANES, shape[0], LANES), F32)],
        name="turn",
    )(flag, own, got)


def pair_kernel(
    lt, wt, gain, wide, narrow, couple, *rest, steps, block, pieces, aliased
):
    panels = rest[:pieces]
    rest = rest[pieces + aliased :]
    out, rq, o0, o1, x0, x1, n0, n1, h0, h1, sems = rest
    nj, width_q, sequences, jc = rq.shape
    channels, flat = wt.shape
    width_p = flat // width_q
    hidden = wide.shape[0]
    lanes = x0.shape[1]
    per = lanes // jc
    sub, step = pl.program_id(0), pl.program_id(1)

    def copies(j):
        outer, seqs = panels[0].shape[0], panels[0].shape[3]
        return [
            pltpu.make_async_copy(
                panels[k].at[z, j],
                rq.at[j, :, pl.ds((k * outer + z) * seqs, seqs), :],
                sems.at[j, k * outer + z],
            )
            for k in range(pieces)
            for z in range(outer)
        ]

    @pl.when((sub == 0) & (step == 0))
    def _():
        for j in range(nj):
            for c in copies(j):
                c.start()

    for j in range(nj):

        @pl.when((sub == j) & (step == 0))
        def _():
            for c in copies(j):
                c.wait()

    xs, ns, hs = (x0, x1), (n0, n1), (h0, h1)

    def outer_pieces(blk, o):
        def piece(k):
            size = block * width_p
            left = lt[pl.ds(pl.multiple_of(blk * size, size), size), :]
            right = jnp.concatenate([rq[sub, k * per + t] for t in range(per)], axis=1)
            r = jnp.dot(left, right, preferred_element_type=F32).astype(BF)
            for t in range(per):
                q = k * per + t
                o[:, q * width_p : (q + 1) * width_p, :] = r[:, t * jc : (t + 1) * jc].reshape(
                    block, width_p, jc
                )

        return [functools.partial(piece, k) for k in range(width_q // per)]

    def rest_pieces(base, o):
        def update(h):
            w = jnp.concatenate([o[h * per + t] for t in range(per)], axis=1)
            u = jnp.dot(wt[...], w, preferred_element_type=F32)
            c = jnp.concatenate(
                [couple[base + h * per + t].astype(F32).T for t in range(per)], axis=1
            )
            xs[h % 2][...] = u + c

        def norm(h):
            x = xs[h % 2][...]
            mean = jnp.mean(x, axis=0, keepdims=True)
            d = x - mean
            var = jnp.mean(d * d, axis=0, keepdims=True)
            ns[h % 2][...] = (d * lax.rsqrt(var + EPS) * gain[...]).astype(BF)

        def widen(h, b):
            r = slice(b * hidden // 2, (b + 1) * hidden // 2)
            hs[h % 2][r, :] = jnp.maximum(
                jnp.dot(wide[r, :], ns[h % 2][...], preferred_element_type=F32), 0.0
            ).astype(BF)

        def shrink(h):
            y = xs[h % 2][...] + jnp.dot(narrow[...], hs[h % 2][...], preferred_element_type=F32)
            for t in range(per):
                out[base + h * per + t] = y[:, t * jc : (t + 1) * jc].T.astype(BF)

        todo = []
        for h in range(0, block // per, 2):
            a, b = h, h + 1
            two = b < block // per
            todo += [functools.partial(update, a)]
            todo += [functools.partial(update, b)] if two else []
            todo += [functools.partial(norm, a), functools.partial(widen, a, 0)]
            todo += [functools.partial(norm, b)] if two else []
            todo += [functools.partial(widen, a, 1)]
            todo += [functools.partial(widen, b, 0)] if two else []
            todo += [functools.partial(shrink, a)]
            todo += [functools.partial(widen, b, 1), functools.partial(shrink, b)] if two else []
        return todo

    def emit(first, second):
        done = 0
        for i, piece in enumerate(second):
            piece()
            want = len(first) * (i + 1) // len(second)
            for k in range(done, want):
                first[k]()
            done = want
        if not second:
            for piece in first:
                piece()

    @pl.when(step == 0)
    def _():
        emit(outer_pieces(0, o0), [])

    emit(outer_pieces(step * 2 + 1, o1), rest_pieces(0, o0))

    @pl.when(step < steps - 1)
    def _():
        emit(outer_pieces(step * 2 + 2, o0), rest_pieces(block, o1))

    @pl.when(step == steps - 1)
    def _():
        emit([], rest_pieces(block, o1))


def pair(lt, panels, wt, gain, wide, narrow, couple, previous, first, width_q):
    tile, res, channels = couple.shape
    outer, nj, _, seqs, jc = panels[0].shape
    sequences = lt.shape[1]
    width_p = lt.shape[0] // tile
    hidden = wide.shape[0]
    block = math.gcd(tile // 2, 8)
    steps = tile // (2 * block)
    lanes = jc * math.gcd(block, 4)
    pair_spec = pl.BlockSpec((2 * block, jc, channels), lambda j, i: (i, first + j, 0))
    any_spec = pl.BlockSpec(memory_space=pl.ANY)
    vmem = pltpu.VMEM
    aliased = previous is not None
    args = [lt, wt, gain, wide, narrow, couple, *panels] + ([previous] if aliased else [])
    return pl.pallas_call(
        functools.partial(
            pair_kernel, steps=steps, block=block, pieces=len(panels), aliased=int(aliased)
        ),
        grid=(nj, steps),
        in_specs=[whole(lt), whole(wt), whole(gain), whole(wide), whole(narrow), pair_spec]
        + [any_spec] * (len(panels) + aliased),
        out_specs=pair_spec,
        out_shape=jax.ShapeDtypeStruct(couple.shape, couple.dtype),
        scratch_shapes=[vmem((nj, width_q, sequences, jc), BF)]
        + [vmem((block, width_q * width_p, jc), BF)] * 2
        + [vmem((channels, lanes), F32)] * 2
        + [vmem((channels, lanes), BF)] * 2
        + [vmem((hidden, lanes), BF)] * 2
        + [pltpu.SemaphoreType.DMA((nj, outer * len(panels)))],
        input_output_aliases={len(args) - 1: 0} if aliased else {},
        compiler_params=pltpu.CompilerParams(vmem_limit_bytes=56 * 1024 * 1024),
        name="pair",
    )(*args)


def on_device(
    homolog_embedding,
    couple_embedding,
    homolog_standardize_factor,
    first_factor_mapping,
    second_factor_mapping,
    contraction_to_couple_mapping,
    couple_standardize_factor,
    widening_matrix,
    narrowing_matrix,
):
    rows, cols = lax.axis_size("rows"), lax.axis_size("cols")
    seqs, res, _ = homolog_embedding.shape
    tile = couple_embedding.shape[0]
    width = first_factor_mapping.shape[1]
    inner = math.gcd(rows, 4)
    outer = rows // inner
    shared = res // tile // inner
    sequences = seqs * rows

    weights = jnp.concatenate([first_factor_mapping, second_factor_mapping], axis=1).T
    left, right = front(
        homolog_embedding, homolog_standardize_factor[None, :], weights, inner, tile
    )
    right = right.reshape(-1, width, seqs, LANES)

    me, core = lax.axis_index("rows"), lax.axis_index("cols")
    my_outer, my_inner = me // inner, me % inner

    def swap(x, k):
        return lax.ppermute(x, "rows", [(r, r ^ k) for r in range(rows)])

    def shift(x, k):
        return lax.ppermute(x, "rows", [(r, (r + k * inner) % rows) for r in range(rows)])

    def gather(block):
        stack = jnp.stack([block] + [shift(block, k) for k in range(1, outer)])
        return [stack] + [swap(stack, k) for k in range(1, inner)]

    def mine(k):
        return lax.dynamic_index_in_dim(left, my_inner ^ k, 0, keepdims=False)

    near = jnp.stack([mine(0)] + [swap(mine(k), k) for k in range(1, inner)], axis=1)
    far = []
    for k in range(outer):
        goal = (my_outer + k) % outer
        block = lax.dynamic_index_in_dim(near, goal % shared, 0, keepdims=False)
        if k:
            pairs = []
            for r in range(rows):
                to = (r + k * inner) % rows
                c = to // inner // shared
                pairs.append((r * cols + c, to * cols + c))
            block = lax.ppermute(block, ("rows", "cols"), pairs)
        far.append(block)
    own = jnp.stack(far)
    got = None
    for m in range(1, cols):
        pairs = []
        for r in range(rows):
            c = r // inner // shared
            pairs.append((r * cols + c, r * cols + (c + m) % cols))
        piece = lax.ppermute(own, ("rows", "cols"), pairs)
        got = piece if got is None else got + piece
    flag = (core == my_outer // shared).astype(jnp.int32).reshape(1)
    lt = turn(flag, own, own if got is None else got, seqs, tile)

    channels = contraction_to_couple_mapping.shape[1]
    wt = contraction_to_couple_mapping.reshape(width, width, channels)
    wt = wt.transpose(2, 1, 0).reshape(channels, width * width)
    wt = (wt.astype(F32) / sequences).astype(BF)
    gain = couple_standardize_factor[:, None]
    wide, narrow = widening_matrix.T, narrowing_matrix.T

    chunks = right.shape[0]
    sizes = CHUNKS if sum(CHUNKS) == chunks else [1] * chunks
    out, first = None, 0
    for size in sizes:
        panels = gather(right[first : first + size])
        out = pair(
            lt, panels, wt, gain, wide, narrow, couple_embedding, out, first, width
        )
        first += size
    return out


CHUNKS = [1, 1, 2]


def solution(mesh):
    return jax.shard_map(
        on_device,
        mesh=mesh,
        in_specs=(P("rows", "cols", None), P("rows", "cols", None)) + (P(),) * 7,
        out_specs=P("rows", "cols", None),
        check_vma=False,
    )
```
